32 devices in a mesh: video: 2 (over x), tm: 16 (over z, y, core).
Axes of the slice: x: 2, y: 2, z: 4, core: 2. Of those that a mesh axis runs over, the one named last changes fastest.
Arguments:
- video: bfloat16 [32, 3, 32, 960], P(('video', 'tm')), parts along dimension 0, may hold values from -6 to 6
- w_in: float32 [32, 3], replicated, may hold values from -3.5 to 3.5
- b_in: float32 [32], replicated, may hold values from -2 to 2
- w_out: float32 [3, 32], replicated, may hold values from -1 to 1
- b_out: float32 [3], replicated, may hold values from -2 to 2
- screen: float32 [3], replicated, may hold values from 0.5 to 2
Outputs:
- consistent: float32 [32, 3, 32, 960], P('video', None, 'tm'), parts along dimension 0
The draws below stay inside these ranges and needn't reach their ends.
There are 2 independent parts, one for each index of `video`. The reference program is written for one: setup_inputs(seed, part) draws one part's arguments, and reference() takes and returns one part's arrays. A program takes and returns all parts, laid end to end along the dimension named above; an argument that names none is the same for every part. Nothing has to cross between parts.
All inputs are finite; a program needn't handle non-finite values.
Results may differ from the reference program's by a relative error of at most 0.0036.
Values may be sent and summed in bfloat16 or wider, within the bound.
A program may use at most 64 MiB of HBM per device.

```python
import math
import jax
import jax.numpy as jnp
from jax import lax

COLS = 960
UNITS = 32
ITERS = 3
FRAMES = 16
ROWS = 32


def draw_video(key, part):
    first_key = jax.random.fold_in(key, 0)
    shape = (FRAMES, 3, ROWS, COLS)
    ramp = 0.5 + jnp.arange(FRAMES, dtype=jnp.float32) / max(FRAMES - 1, 1)
    base = jnp.clip(jax.random.normal(first_key, shape, jnp.float32), -4.0, 4.0)
    return (base * ramp[:, None, None, None]).astype(jnp.bfloat16)


def noise(key, shape, width, reach, kind=jnp.bfloat16):
    values = width * jax.random.normal(key, shape, jnp.float32)
    return jnp.clip(values, min=-reach, max=reach).astype(kind)


def setup_inputs(seed: int = 0, part: int = 0) -> dict:
    splits = jax.random.split(jax.random.key(seed), 7)
    part_keys = jax.random.split(jax.random.fold_in(splits[6], part), 7)
    video = draw_video(jax.random.fold_in(jax.random.fold_in(splits[6], part), 71), part)
    w_in = noise(splits[1], (UNITS, 3), 3 ** -0.5, 3.5, jnp.float32)
    b_in = noise(splits[2], (UNITS,), 0.5, 2.0, jnp.float32)
    w_out = noise(splits[3], (3, UNITS), UNITS ** -0.5, 1.0, jnp.float32)
    b_out = noise(splits[4], (3,), 0.5, 2.0, jnp.float32)
    screen = jnp.clip(jnp.exp(jax.random.uniform(splits[5], (3,), jnp.float32, math.log(0.5), math.log(2.0))), 0.5, 2.0)
    return {"video": video, "w_in": w_in, "b_in": b_in, "w_out": w_out, "b_out": b_out, "screen": screen}


highest = lax.Precision.HIGHEST


def grade_frame(frame_in, w_in, b_in, w_out, b_out, screen):
    pixels = frame_in.astype(jnp.float32)
    before = jnp.einsum("jc,crw->jrw", w_in, pixels, precision=highest) + b_in[:, None, None]
    graded = pixels + jnp.einsum("cj,jrw->crw", w_out, jax.nn.silu(before), precision=highest) + b_out[:, None, None]
    padded = jnp.pad(graded, ((0, 0), (1, 1), (1, 1)))
    beside_all = padded[:, 2:, 1:-1] + padded[:, :-2, 1:-1] + padded[:, 1:-1, 2:] + padded[:, 1:-1, :-2]
    return ((screen[:, None, None] + 4.0) * graded - beside_all).astype(jnp.bfloat16)


def neighbours(padded):
    total = padded[2:, :, 1:-1, 1:-1] + padded[:-2, :, 1:-1, 1:-1]
    total = total + padded[1:-1, :, 2:, 1:-1] + padded[1:-1, :, :-2, 1:-1]
    total = total + padded[1:-1, :, 1:-1, 2:] + padded[1:-1, :, 1:-1, :-2]
    return total


def operate(field, screen):
    padded = jnp.pad(field, ((1, 1), (0, 0), (1, 1), (1, 1)))
    return (6.0 + screen[None, :, None, None]) * field - neighbours(padded)


def channel_dot(left, right):
    return jnp.sum(left * right, axis=(0, 2, 3))


def widen(values):
    return values[None, :, None, None]


def reference(video, w_in, b_in, w_out, b_out, screen):
    target = lax.map(lambda frame_in: grade_frame(frame_in, w_in, b_in, w_out, b_out, screen), video)
    source = target.astype(jnp.float32)
    solution = jnp.zeros_like(source)
    residual = source
    direction = source
    norm_now = channel_dot(residual, residual)
    for sweep_index in range(ITERS):
        image = operate(direction, screen)
        alpha = norm_now / channel_dot(direction, image)
        solution = solution + widen(alpha) * direction
        residual = residual - widen(alpha) * image
        norm_next = channel_dot(residual, residual)
        direction = residual + widen(norm_next / norm_now) * direction
        norm_now = norm_next
    return solution
```

```python
import functools

import jax
import jax.numpy as jnp
from jax import lax
from jax.experimental import pallas as pl
from jax.experimental.pallas import tpu as pltpu
from jax.sharding import PartitionSpec as P

ITERS = 3
LANES = 128
HELD = 1
HALO = ITERS + 1


def blocks_of(count, size):
    return [(start, min(size, count - start)) for start in range(0, count, size)]


def partner(index, step, count):
    if count & (count - 1):
        return lax.rem(index + count // 2 + step, count)
    mask, found, bit = count - 1 - step, 0, 1
    while bit < count:
        found = found + lax.rem(index // bit + mask // bit, 2) * bit
        bit *= 2
    return found


def shifted(field, axis, step):
    size = field.shape[axis]
    index = lax.broadcasted_iota(jnp.int32, field.shape, axis)
    moved = pltpu.roll(field, 1 if step == 1 else size - 1, axis)
    return jnp.where(index == (0 if step == 1 else size - 1), 0.0, moved)


def coefficients(m):
    a0 = m[0] / m[1]
    rr1 = m[0] - 2.0 * a0 * m[1] + a0 * a0 * m[2]
    p10, p11 = 1.0 + rr1 / m[0], -a0
    a1 = rr1 / (p10 * p10 * m[1] + 2.0 * p10 * p11 * m[2] + p11 * p11 * m[3])
    r1, r2 = -a0 - a1 * p10, -a1 * p11
    rr2 = m[0] + r1 * r1 * m[2] + r2 * r2 * m[4] + 2.0 * (r1 * m[1] + r2 * m[2] + r1 * r2 * m[3])
    beta = rr2 / rr1
    p20, p21, p22 = 1.0 + beta * p10, r1 + beta * p11, r2
    bottom = (
        p20 * p20 * m[1]
        + p21 * p21 * m[3]
        + p22 * p22 * m[5]
        + 2.0 * (p20 * p21 * m[2] + p20 * p22 * m[3] + p21 * p22 * m[4])
    )
    a2 = rr2 / bottom
    return a0 + a1 * p10 + a2 * p20, a1 * p11 + a2 * p21, a2 * p22


def kernel(
    count,
    video_hbm, w_in_hbm, b_in_hbm, w_out_hbm, b_out_hbm, screen_hbm,
    recv2,
    video_ref, w_in_ref, b_in_ref, w_out_ref, b_out_ref, screen_ref, load_sem,
    wide, pieces, packed, send1, recv1, flat, power0, power1, power2,
    mine, sums, send2,
    send1_sem, recv1_sem, sum_send_sem, sum_recv_sem, send2_sem, recv2_sem, local_sem,
):
    me = lax.axis_index("tm")
    chips = count // 2
    chip, core = lax.rem(me, chips), me // chips
    _, channels, rows, cols = video_ref.shape
    units = w_in_ref.shape[1]
    frames = count
    own = cols // chips
    half = rows // 2
    window = half + ITERS
    chunk = send1.shape[1]
    band = rows // count
    bands = count // 2

    barrier = pltpu.get_barrier_semaphore()

    def greet(step, carry):
        pl.semaphore_signal(barrier, inc=1, device_id={"tm": lax.rem(me + step, count)})
        return carry

    loads = [
        pltpu.make_async_copy(source, dest, load_sem.at[i])
        for i, (source, dest) in enumerate(
            (
                (video_hbm, video_ref),
                (w_in_hbm, w_in_ref),
                (b_in_hbm, b_in_ref),
                (w_out_hbm, w_out_ref),
                (b_out_hbm, b_out_ref),
                (screen_hbm, screen_ref),
            )
        )
    ]
    for load in loads:
        load.start()
    lax.fori_loop(1, count, greet, 0)
    for load in loads:
        load.wait()

    tiles = wide.shape[2] // LANES
    for c in range(channels):
        wide[c, :, :LANES] = jnp.zeros((rows, LANES), jnp.float32)
        for t in range(1 + cols // LANES, tiles):
            wide[c, :, t * LANES:(t + 1) * LANES] = jnp.zeros((rows, LANES), jnp.float32)
        wide[c, :, LANES:LANES + cols] = video_ref[0, c].astype(jnp.float32)
    lane2 = lax.broadcasted_iota(jnp.int32, (rows, LANES), 1)
    for k in range(chips):
        tile, offset = divmod(LANES + own * k - HALO, LANES)
        for c in range(channels):
            first = wide[c, :, tile * LANES:(tile + 1) * LANES]
            if offset:
                second = wide[c, :, (tile + 1) * LANES:(tile + 2) * LANES]
                first = pltpu.roll(first, LANES - offset, 1)
                second = pltpu.roll(second, LANES - offset, 1)
                first = jnp.where(lane2 < LANES - offset, first, second)
            pieces[k, c] = first
    packed[...] = jnp.zeros_like(packed)

    def grade(k):
        column = lane2 + (own * k - HALO)
        inside = jnp.logical_and(column >= 0, column < cols)
        parts = [[] for _ in range(channels)]
        for start, size in blocks_of(rows, 32):
            pixels = [pieces[k, c, start:start + size, :] for c in range(channels)]
            total = [pixels[c] + b_out_ref[c] for c in range(channels)]
            for j in range(units):
                h = pixels[0] * (0.5 * w_in_ref[0, j]) + 0.5 * b_in_ref[j]
                for c in range(1, channels):
                    h = h + pixels[c] * (0.5 * w_in_ref[c, j])
                act = h * jnp.tanh(h) + h
                for c in range(channels):
                    total[c] = total[c] + act * w_out_ref[c, j]
            for c in range(channels):
                parts[c].append(total[c])
        for c in range(channels):
            graded = parts[c][0] if len(parts[c]) == 1 else jnp.concatenate(parts[c], 0)
            graded = jnp.where(inside, graded, 0.0)
            beside = shifted(graded, 0, 1) + shifted(graded, 0, -1)
            beside = beside + pltpu.roll(graded, 1, 1) + pltpu.roll(graded, LANES - 1, 1)
            target = jnp.where(inside, (screen_ref[c] + 4.0) * graded - beside, 0.0)
            packed[0, c * window:(c + 1) * window, :] = target[:window]
            packed[1, c * window:(c + 1) * window, :] = target[rows - window:]

    def copy1(dest):
        return pltpu.make_async_remote_copy(
            src_ref=send1.at[dest],
            dst_ref=recv1.at[me],
            send_sem=send1_sem.at[dest],
            recv_sem=recv1_sem.at[me],
            device_id={"tm": dest},
        )

    def arrival1(source):
        return pltpu.make_async_remote_copy(
            src_ref=send1.at[source],
            dst_ref=recv1.at[source],
            send_sem=send1_sem.at[source],
            recv_sem=recv1_sem.at[source],
            device_id={"tm": source},
        )

    held = min(HELD, chips - 1)

    def launch(k):
        for side in range(2):
            dest = side * chips + k

            @pl.when(dest != me)
            def _():
                copy1(dest).start()

    def make(step, carry):
        k = lax.rem(chip + chips // 2 + step, chips)
        grade(k)
        for side in range(2):
            send1[side * chips + k] = packed[side].astype(jnp.bfloat16)

        @pl.when(step == held)
        def _():
            pl.semaphore_wait(barrier, count - 1)
            for earlier in range(held):
                launch(lax.rem(chip + chips // 2 + earlier, chips))

        @pl.when(step >= held)
        def _():
            launch(k)

        return carry

    lax.fori_loop(0, chips, make, 0)
    recv1[me] = send1[me]

    def land(step, carry):
        source = lax.rem(me + step, count)

        @pl.when(step > 0)
        def _():
            arrival1(source).wait_recv()

        flat[pl.ds(pl.multiple_of(source * chunk, chunk), chunk), :] = recv1[source].astype(jnp.float32)
        return carry

    lax.fori_loop(0, count, land, 0)

    lane = lax.broadcasted_iota(jnp.int32, (1, frames, LANES), 2)
    column = lane + (own * chip - HALO)
    inside = jnp.logical_and(column >= 0, column < cols)
    owned = jnp.logical_and(lane >= HALO, lane < HALO + own)
    frame = lax.broadcasted_iota(jnp.int32, (1, frames, LANES), 1)

    for power in (power0, power1, power2):
        for c in range(channels):
            power[c, 0] = jnp.zeros((frames, LANES), jnp.float32)
            power[c, window + 1] = jnp.zeros((frames, LANES), jnp.float32)
    for c in range(channels):
        for r in range(window):
            power0[c, r + 1] = flat[pl.ds(c * window + r, frames, chunk), :]

    def operate(ref, c, start, size):
        whole = ref[c, pl.ds(start, size + 2)]
        centre = whole[1:size + 1]
        total = whole[:size] + whole[2:]
        total = total + pltpu.roll(centre, 1, 2) + pltpu.roll(centre, LANES - 1, 2)
        before = jnp.where(frame == 0, 0.0, pltpu.roll(centre, 1, 1))
        after = jnp.where(frame == frames - 1, 0.0, pltpu.roll(centre, frames - 1, 1))
        total = total + before + after
        return centre, (6.0 + screen_ref[c]) * centre - total

    shift = core * ITERS
    for ref, result in ((power0, power1), (power1, power2)):
        def apply(c, carry, ref=ref, result=result):
            for start, size in blocks_of(window, 4):
                _, image = operate(ref, c, start, size)
                result[c, start + 1:start + 1 + size] = jnp.where(inside, image, 0.0)
            return carry

        lax.fori_loop(0, channels, apply, 0)

    lane1 = lax.broadcasted_iota(jnp.int32, (1, LANES), 1)

    def moments(c, row):
        acc = [jnp.zeros((frames, LANES), jnp.float32) for _ in range(6)]
        for start, size in blocks_of(half, 4):
            v0 = power0[c, pl.ds(shift + start + 1, size)]
            v1 = power1[c, pl.ds(shift + start + 1, size)]
            v2, v3 = operate(power2, c, shift + start, size)
            for i, (left, right) in enumerate(
                ((v0, v0), (v0, v1), (v1, v1), (v1, v2), (v2, v2), (v2, v3))
            ):
                acc[i] = acc[i] + jnp.sum(left * right, axis=0)
        for i in range(6):
            value = jnp.sum(jnp.where(owned[0], acc[i], 0.0), axis=0, keepdims=True)
            value = jnp.sum(value, axis=1, keepdims=True)
            row = jnp.where(lane1 == c * 8 + i, value, row)
        return row

    mine[0] = lax.fori_loop(0, channels, moments, jnp.zeros((1, LANES), jnp.float32))

    def sum_copy(other, slot):
        return pltpu.make_async_remote_copy(
            src_ref=mine.at[0],
            dst_ref=sums.at[slot],
            send_sem=sum_send_sem.at[other],
            recv_sem=sum_recv_sem.at[slot],
            device_id={"tm": other},
        )

    def tell(step, carry):
        other = partner(me, step, count)

        @pl.when(other != me)
        def _():
            sum_copy(other, me).start()

        return carry

    lax.fori_loop(0, count, tell, 0)
    sums[me] = mine[0]

    def hear(step, carry):
        other = lax.rem(me + step, count)
        sum_copy(other, other).wait_recv()
        return carry

    lax.fori_loop(1, count, hear, 0)
    total = sums[0]
    for other in range(1, count):
        total = total + sums[other]
    moment = [total if i == 0 else pltpu.roll(total, LANES - i, 1) for i in range(6)]
    weights = coefficients(moment)
    spread = [
        [
            jnp.sum(jnp.where(lane1 == c * 8, w, 0.0), axis=1, keepdims=True).reshape(1, 1, 1)
            for w in weights
        ]
        for c in range(channels)
    ]

    def copy2(slot, dest, where):
        return pltpu.make_async_remote_copy(
            src_ref=send2.at[slot],
            dst_ref=recv2.at[where],
            send_sem=send2_sem.at[slot],
            recv_sem=recv2_sem.at[where],
            device_id={"tm": dest},
        )

    def give(step, carry):
        slot = lax.rem(lax.rem(me, bands) + bands // 2 + step, bands)
        dest = core * bands + slot
        start = shift + slot * band + 1
        for c in range(channels):
            result = spread[c][0] * power0[c, pl.ds(start, band)]
            result = result + spread[c][1] * power1[c, pl.ds(start, band)]
            result = result + spread[c][2] * power2[c, pl.ds(start, band)]
            send2[slot, c] = result.astype(jnp.bfloat16)

        @pl.when(dest != me)
        def _():
            copy2(slot, dest, chip).start()

        @pl.when(dest == me)
        def _():
            pltpu.make_async_copy(send2.at[slot], recv2.at[chip], local_sem.at[1]).start()

        return carry

    lax.fori_loop(0, bands, give, 0)

    def drain(step, carry):
        other = lax.rem(me + step, count)
        copy1(other).wait_send()
        sum_copy(other, me).wait_send()
        return carry

    lax.fori_loop(1, count, drain, 0)

    def take(k, carry):
        giver = core * chips + k

        @pl.when(giver != me)
        def _():
            copy2(0, giver, k).wait_recv()

        @pl.when(giver == me)
        def _():
            pltpu.make_async_copy(send2.at[0], recv2.at[k], local_sem.at[1]).wait()

        return carry

    lax.fori_loop(0, chips, take, 0)
    def finish(slot, carry):
        dest = core * bands + slot

        @pl.when(dest != me)
        def _():
            copy2(slot, dest, chip).wait_send()

        return carry

    lax.fori_loop(0, bands, finish, 0)


def assemble(own, recv2, out_ref):
    frames, channels, band, cols = out_ref.shape
    for start, size in blocks_of(cols, LANES):
        column = start + lax.broadcasted_iota(jnp.int32, (frames, LANES), 1)
        for c in range(channels):
            for r in range(band):
                tile = jnp.zeros((frames, LANES), jnp.float32)
                for k in range(start // own, (start + size - 1) // own + 1):
                    piece = recv2[k, c, r].astype(jnp.float32)
                    turn = (own * k - HALO - start) % LANES
                    piece = pltpu.roll(piece, turn, 1) if turn else piece
                    tile = jnp.where(column >= own * k, piece, tile)
                out_ref[:, c, r, start:start + size] = tile[:, :size]


def shards(count, video, w_in, b_in, w_out, b_out, screen):
    _, channels, rows, cols = video.shape
    chips, band = count // 2, rows // count
    window = rows // 2 + ITERS
    chunk = -(-channels * window // 16) * 16
    f32, bf16 = jnp.float32, jnp.bfloat16
    field = pltpu.VMEM((channels, window + 2, count, LANES), f32)
    dma = pltpu.SemaphoreType.DMA
    out = pl.pallas_call(
        functools.partial(kernel, count),
        out_shape=jax.ShapeDtypeStruct((chips, channels, band, count, LANES), bf16),
        in_specs=[pl.BlockSpec(memory_space=pl.ANY)] * 6,
        out_specs=pl.BlockSpec(memory_space=pl.ANY),
        scratch_shapes=[
            pltpu.VMEM(video.shape, video.dtype),
            pltpu.SMEM(w_in.shape[::-1], f32),
            pltpu.SMEM(b_in.shape, f32),
            pltpu.SMEM(w_out.shape, f32),
            pltpu.SMEM(b_out.shape, f32),
            pltpu.SMEM(screen.shape, f32),
            dma((6,)),
            pltpu.VMEM((channels, rows, (-(-cols // LANES) + 2) * LANES), f32),
            pltpu.VMEM((chips, channels, rows, LANES), f32),
            pltpu.VMEM((2, chunk, LANES), f32),
            pltpu.VMEM((count, chunk, LANES), bf16),
            pltpu.VMEM((count, chunk, LANES), bf16),
            pltpu.VMEM((count * chunk, LANES), f32),
            field, field, field,
            pltpu.VMEM((1, 1, LANES), f32),
            pltpu.VMEM((count, 1, LANES), f32),
            pltpu.VMEM((count // 2, channels, band, count, LANES), bf16),
            dma((count,)), dma((count,)), dma((count,)), dma((count,)),
            dma((count // 2,)), dma((chips,)), dma((2,)),
        ],
        compiler_params=pltpu.CompilerParams(collective_id=0, has_side_effects=True),
    )(video, w_in.T, b_in, w_out, b_out, screen)
    return pl.pallas_call(
        functools.partial(assemble, cols // chips),
        out_shape=jax.ShapeDtypeStruct((count, channels, band, cols), f32),
        in_specs=[pl.BlockSpec(memory_space=pltpu.VMEM)],
        out_specs=pl.BlockSpec(memory_space=pltpu.VMEM),
    )(out)


def solution(mesh):
    in_specs = (P(("video", "tm"), None, None, None), P(), P(), P(), P(), P())
    out_specs = P("video", None, "tm", None)
    body = functools.partial(shards, mesh.shape["tm"])
    return jax.shard_map(body, mesh=mesh, in_specs=in_specs, out_specs=out_specs, check_vma=False)
```

```python
import functools

import jax
import jax.numpy as jnp
from jax import lax
from jax.experimental import pallas as pl
from jax.experimental.pallas import tpu as pltpu
from jax.sharding import PartitionSpec as P

ITERS = 3
LANES = 128
HELD = 1
HALO = ITERS + 1


def blocks_of(count, size):
    return [(start, min(size, count - start)) for start in range(0, count, size)]


def partner(index, step, count):
    if count & (count - 1):
        return lax.rem(index + count // 2 + step, count)
    mask, found, bit = count - 1 - step, 0, 1
    while bit < count:
        found = found + lax.rem(index // bit + mask // bit, 2) * bit
        bit *= 2
    return found


def shifted(field, axis, step):
    size = field.shape[axis]
    index = lax.broadcasted_iota(jnp.int32, field.shape, axis)
    moved = pltpu.roll(field, 1 if step == 1 else size - 1, axis)
    return jnp.where(index == (0 if step == 1 else size - 1), 0.0, moved)


def coefficients(m):
    a0 = m[0] / m[1]
    rr1 = m[0] - 2.0 * a0 * m[1] + a0 * a0 * m[2]
    p10, p11 = 1.0 + rr1 / m[0], -a0
    a1 = rr1 / (p10 * p10 * m[1] + 2.0 * p10 * p11 * m[2] + p11 * p11 * m[3])
    r1, r2 = -a0 - a1 * p10, -a1 * p11
    rr2 = m[0] + r1 * r1 * m[2] + r2 * r2 * m[4] + 2.0 * (r1 * m[1] + r2 * m[2] + r1 * r2 * m[3])
    beta = rr2 / rr1
    p20, p21, p22 = 1.0 + beta * p10, r1 + beta * p11, r2
    bottom = (
        p20 * p20 * m[1]
        + p21 * p21 * m[3]
        + p22 * p22 * m[5]
        + 2.0 * (p20 * p21 * m[2] + p20 * p22 * m[3] + p21 * p22 * m[4])
    )
    a2 = rr2 / bottom
    return a0 + a1 * p10 + a2 * p20, a1 * p11 + a2 * p21, a2 * p22


def kernel(
    count,
    video_hbm, w_in_hbm, b_in_hbm, w_out_hbm, b_out_hbm, screen_hbm,
    recv2,
    video_ref, w_in_ref, b_in_ref, w_out_ref, b_out_ref, screen_ref, load_sem,
    wide, pieces, packed, send1, recv1, flat, power0, power1, power2,
    mine, sums, send2,
    send1_sem, recv1_sem, sum_send_sem, sum_recv_sem, send2_sem, recv2_sem, local_sem,
):
    me = lax.axis_index("tm")
    chips = count // 2
    chip, core = lax.rem(me, chips), me // chips
    _, channels, rows, cols = video_ref.shape
    units = w_in_ref.shape[1]
    frames = count
    own = cols // chips
    half = rows // 2
    window = half + ITERS
    chunk = send1.shape[1]
    band = rows // count
    bands = count // 2

    barrier = pltpu.get_barrier_semaphore()

    def greet(step, carry):
        pl.semaphore_signal(barrier, inc=1, device_id={"tm": lax.rem(me + step, count)})
        return carry

    lax.fori_loop(1, count, greet, 0)

    loads = [
        pltpu.make_async_copy(source, dest, load_sem.at[i])
        for i, (source, dest) in enumerate(
            (
                (video_hbm, video_ref),
                (w_in_hbm, w_in_ref),
                (b_in_hbm, b_in_ref),
                (w_out_hbm, w_out_ref),
                (b_out_hbm, b_out_ref),
                (screen_hbm, screen_ref),
            )
        )
    ]
    for load in loads:
        load.start()
    for load in loads:
        load.wait()

    tiles = wide.shape[2] // LANES
    for c in range(channels):
        wide[c, :, :LANES] = jnp.zeros((rows, LANES), jnp.float32)
        for t in range(1 + cols // LANES, tiles):
            wide[c, :, t * LANES:(t + 1) * LANES] = jnp.zeros((rows, LANES), jnp.float32)
        wide[c, :, LANES:LANES + cols] = video_ref[0, c].astype(jnp.float32)
    lane2 = lax.broadcasted_iota(jnp.int32, (rows, LANES), 1)
    for k in range(chips):
        tile, offset = divmod(LANES + own * k - HALO, LANES)
        for c in range(channels):
            first = wide[c, :, tile * LANES:(tile + 1) * LANES]
            if offset:
                second = wide[c, :, (tile + 1) * LANES:(tile + 2) * LANES]
                first = pltpu.roll(first, LANES - offset, 1)
                second = pltpu.roll(second, LANES - offset, 1)
                first = jnp.where(lane2 < LANES - offset, first, second)
            pieces[k, c] = first
    packed[...] = jnp.zeros_like(packed)

    def grade(k):
        column = lane2 + (own * k - HALO)
        inside = jnp.logical_and(column >= 0, column < cols)
        parts = [[] for _ in range(channels)]
        for start, size in blocks_of(rows, 32):
            pixels = [pieces[k, c, start:start + size, :] for c in range(channels)]
            total = [pixels[c] + b_out_ref[c] for c in range(channels)]
            for j in range(units):
                h = pixels[0] * (0.5 * w_in_ref[0, j]) + 0.5 * b_in_ref[j]
                for c in range(1, channels):
                    h = h + pixels[c] * (0.5 * w_in_ref[c, j])
                act = h * jnp.tanh(h) + h
                for c in range(channels):
                    total[c] = total[c] + act * w_out_ref[c, j]
            for c in range(channels):
                parts[c].append(total[c])
        for c in range(channels):
            graded = parts[c][0] if len(parts[c]) == 1 else jnp.concatenate(parts[c], 0)
            graded = jnp.where(inside, graded, 0.0)
            beside = shifted(graded, 0, 1) + shifted(graded, 0, -1)
            beside = beside + pltpu.roll(graded, 1, 1) + pltpu.roll(graded, LANES - 1, 1)
            target = jnp.where(inside, (screen_ref[c] + 4.0) * graded - beside, 0.0)
            packed[0, c * window:(c + 1) * window, :] = target[:window]
            packed[1, c * window:(c + 1) * window, :] = target[rows - window:]

    def copy1(dest):
        return pltpu.make_async_remote_copy(
            src_ref=send1.at[dest],
            dst_ref=recv1.at[me],
            send_sem=send1_sem.at[dest],
            recv_sem=recv1_sem.at[me],
            device_id={"tm": dest},
        )

    def arrival1(source):
        return pltpu.make_async_remote_copy(
            src_ref=send1.at[source],
            dst_ref=recv1.at[source],
            send_sem=send1_sem.at[source],
            recv_sem=recv1_sem.at[source],
            device_id={"tm": source},
        )

    held = min(HELD, chips - 1)

    def launch(k):
        for side in range(2):
            dest = side * chips + k

            @pl.when(dest != me)
            def _():
                copy1(dest).start()

    def make(step, carry):
        k = lax.rem(chip + chips // 2 + step, chips)
        grade(k)
        for side in range(2):
            send1[side * chips + k] = packed[side].astype(jnp.bfloat16)

        @pl.when(step == held)
        def _():
            pl.semaphore_wait(barrier, count - 1)
            for earlier in range(held):
                launch(lax.rem(chip + chips // 2 + earlier, chips))

        @pl.when(step >= held)
        def _():
            launch(k)

        return carry

    lax.fori_loop(0, chips, make, 0)
    recv1[me] = send1[me]

    def land(step, carry):
        source = lax.rem(me + step, count)

        @pl.when(step > 0)
        def _():
            arrival1(source).wait_recv()

        flat[pl.ds(pl.multiple_of(source * chunk, chunk), chunk), :] = recv1[source].astype(jnp.float32)
        return carry

    lax.fori_loop(0, count, land, 0)

    lane = lax.broadcasted_iota(jnp.int32, (1, frames, LANES), 2)
    column = lane + (own * chip - HALO)
    inside = jnp.logical_and(column >= 0, column < cols)
    owned = jnp.logical_and(lane >= HALO, lane < HALO + own)
    frame = lax.broadcasted_iota(jnp.int32, (1, frames, LANES), 1)

    for power in (power0, power1, power2):
        for c in range(channels):
            power[c, 0] = jnp.zeros((frames, LANES), jnp.float32)
            power[c, window + 1] = jnp.zeros((frames, LANES), jnp.float32)
    for c in range(channels):
        for r in range(window):
            power0[c, r + 1] = flat[pl.ds(c * window + r, frames, chunk), :]

    def operate(ref, c, start, size):
        whole = ref[c, pl.ds(start, size + 2)]
        centre = whole[1:size + 1]
        total = whole[:size] + whole[2:]
        total = total + pltpu.roll(centre, 1, 2) + pltpu.roll(centre, LANES - 1, 2)
        before = jnp.where(frame == 0, 0.0, pltpu.roll(centre, 1, 1))
        after = jnp.where(frame == frames - 1, 0.0, pltpu.roll(centre, frames - 1, 1))
        total = total + before + after
        return centre, (6.0 + screen_ref[c]) * centre - total

    shift = core * ITERS
    for ref, result in ((power0, power1), (power1, power2)):
        def apply(c, carry, ref=ref, result=result):
            for start, size in blocks_of(window, 4):
                _, image = operate(ref, c, start, size)
                result[c, start + 1:start + 1 + size] = jnp.where(inside, image, 0.0)
            return carry

        lax.fori_loop(0, channels, apply, 0)

    lane1 = lax.broadcasted_iota(jnp.int32, (1, LANES), 1)

    def moments(c, row):
        acc = [jnp.zeros((frames, LANES), jnp.float32) for _ in range(6)]
        for start, size in blocks_of(half, 4):
            v0 = power0[c, pl.ds(shift + start + 1, size)]
            v1 = power1[c, pl.ds(shift + start + 1, size)]
            v2, v3 = operate(power2, c, shift + start, size)
            for i, (left, right) in enumerate(
                ((v0, v0), (v0, v1), (v1, v1), (v1, v2), (v2, v2), (v2, v3))
            ):
                acc[i] = acc[i] + jnp.sum(left * right, axis=0)
        for i in range(6):
            value = jnp.sum(jnp.where(owned[0], acc[i], 0.0), axis=0, keepdims=True)
            value = jnp.sum(value, axis=1, keepdims=True)
            row = jnp.where(lane1 == c * 8 + i, value, row)
        return row

    mine[0] = lax.fori_loop(0, channels, moments, jnp.zeros((1, LANES), jnp.float32))

    def sum_copy(other, slot):
        return pltpu.make_async_remote_copy(
            src_ref=mine.at[0],
            dst_ref=sums.at[slot],
            send_sem=sum_send_sem.at[other],
            recv_sem=sum_recv_sem.at[slot],
            device_id={"tm": other},
        )

    def tell(step, carry):
        other = partner(me, step, count)

        @pl.when(other != me)
        def _():
            sum_copy(other, me).start()

        return carry

    lax.fori_loop(0, count, tell, 0)
    sums[me] = mine[0]

    def hear(step, carry):
        other = lax.rem(me + step, count)
        sum_copy(other, other).wait_recv()
        return carry

    lax.fori_loop(1, count, hear, 0)
    total = sums[0]
    for other in range(1, count):
        total = total + sums[other]
    moment = [total if i == 0 else pltpu.roll(total, LANES - i, 1) for i in range(6)]
    weights = coefficients(moment)
    spread = [
        [
            jnp.sum(jnp.where(lane1 == c * 8, w, 0.0), axis=1, keepdims=True).reshape(1, 1, 1)
            for w in weights
        ]
        for c in range(channels)
    ]

    def copy2(slot, dest, where):
        return pltpu.make_async_remote_copy(
            src_ref=send2.at[slot],
            dst_ref=recv2.at[where],
            send_sem=send2_sem.at[slot],
            recv_sem=recv2_sem.at[where],
            device_id={"tm": dest},
        )

    def give(step, carry):
        slot = step
        dest = core * bands + slot
        start = shift + slot * band + 1
        for c in range(channels):
            result = spread[c][0] * power0[c, pl.ds(start, band)]
            result = result + spread[c][1] * power1[c, pl.ds(start, band)]
            result = result + spread[c][2] * power2[c, pl.ds(start, band)]
            send2[slot, c] = result.astype(jnp.bfloat16)

        @pl.when(dest != me)
        def _():
            copy2(slot, dest, chip).start()

        @pl.when(dest == me)
        def _():
            pltpu.make_async_copy(send2.at[slot], recv2.at[chip], local_sem.at[1]).start()

        return carry

    lax.fori_loop(0, bands, give, 0)

    def drain(step, carry):
        other = lax.rem(me + step, count)
        copy1(other).wait_send()
        sum_copy(other, me).wait_send()
        return carry

    lax.fori_loop(1, count, drain, 0)

    def take(k, carry):
        giver = core * chips + k

        @pl.when(giver != me)
        def _():
            copy2(0, giver, k).wait_recv()

        @pl.when(giver == me)
        def _():
            pltpu.make_async_copy(send2.at[0], recv2.at[k], local_sem.at[1]).wait()

        return carry

    lax.fori_loop(0, chips, take, 0)
    def finish(slot, carry):
        dest = core * bands + slot

        @pl.when(dest != me)
        def _():
            copy2(slot, dest, chip).wait_send()

        return carry

    lax.fori_loop(0, bands, finish, 0)


def assemble(own, recv2, out_ref):
    frames, channels, band, cols = out_ref.shape
    for start, size in blocks_of(cols, LANES):
        column = start + lax.broadcasted_iota(jnp.int32, (frames, LANES), 1)
        for c in range(channels):
            for r in range(band):
                tile = jnp.zeros((frames, LANES), jnp.float32)
                for k in range(start // own, (start + size - 1) // own + 1):
                    piece = recv2[k, c, r].astype(jnp.float32)
                    turn = (own * k - HALO - start) % LANES
                    piece = pltpu.roll(piece, turn, 1) if turn else piece
                    tile = jnp.where(column >= own * k, piece, tile)
                out_ref[:, c, r, start:start + size] = tile[:, :size]


def shards(count, video, w_in, b_in, w_out, b_out, screen):
    _, channels, rows, cols = video.shape
    chips, band = count // 2, rows // count
    window = rows // 2 + ITERS
    chunk = -(-channels * window // 16) * 16
    f32, bf16 = jnp.float32, jnp.bfloat16
    field = pltpu.VMEM((channels, window + 2, count, LANES), f32)
    dma = pltpu.SemaphoreType.DMA
    out = pl.pallas_call(
        functools.partial(kernel, count),
        out_shape=jax.ShapeDtypeStruct((chips, channels, band, count, LANES), bf16),
        in_specs=[pl.BlockSpec(memory_space=pl.ANY)] * 6,
        out_specs=pl.BlockSpec(memory_space=pl.ANY),
        scratch_shapes=[
            pltpu.VMEM(video.shape, video.dtype),
            pltpu.SMEM(w_in.shape[::-1], f32),
            pltpu.SMEM(b_in.shape, f32),
            pltpu.SMEM(w_out.shape, f32),
            pltpu.SMEM(b_out.shape, f32),
            pltpu.SMEM(screen.shape, f32),
            dma((6,)),
            pltpu.VMEM((channels, rows, (-(-cols // LANES) + 2) * LANES), f32),
            pltpu.VMEM((chips, channels, rows, LANES), f32),
            pltpu.VMEM((2, chunk, LANES), f32),
            pltpu.VMEM((count, chunk, LANES), bf16),
            pltpu.VMEM((count, chunk, LANES), bf16),
            pltpu.VMEM((count * chunk, LANES), f32),
            field, field, field,
            pltpu.VMEM((1, 1, LANES), f32),
            pltpu.VMEM((count, 1, LANES), f32),
            pltpu.VMEM((count // 2, channels, band, count, LANES), bf16),
            dma((count,)), dma((count,)), dma((count,)), dma((count,)),
            dma((count // 2,)), dma((chips,)), dma((2,)),
        ],
        compiler_params=pltpu.CompilerParams(collective_id=0, has_side_effects=True, vmem_limit_bytes=60 << 20),
    )(*[pltpu.with_memory_space_constraint(a, pltpu.HBM) for a in (video, w_in.T, b_in, w_out, b_out, screen)])
    return pl.pallas_call(
        functools.partial(assemble, cols // chips),
        out_shape=jax.ShapeDtypeStruct((count, channels, band, cols), f32),
        in_specs=[pl.BlockSpec(memory_space=pltpu.VMEM)],
        out_specs=pl.BlockSpec(memory_space=pltpu.VMEM),
        compiler_params=pltpu.CompilerParams(vmem_limit_bytes=8 << 20),
    )(out)


def solution(mesh):
    in_specs = (P(("video", "tm"), None, None, None), P(), P(), P(), P(), P())
    out_specs = P("video", None, "tm", None)
    body = functools.partial(shards, mesh.shape["tm"])
    return jax.shard_map(body, mesh=mesh, in_specs=in_specs, out_specs=out_specs, check_vma=False)
```

```python
import functools

import jax
import jax.numpy as jnp
from jax import lax
from jax.experimental import pallas as pl
from jax.experimental.pallas import tpu as pltpu
from jax.sharding import PartitionSpec as P

ITERS = 3
LANES = 128
HELD = 1
HALO = ITERS + 1


def blocks_of(count, size):
    return [(start, min(size, count - start)) for start in range(0, count, size)]


def partner(index, step, count):
    if count & (count - 1):
        return lax.rem(index + count // 2 + step, count)
    mask, found, bit = count - 1 - step, 0, 1
    while bit < count:
        found = found + lax.rem(index // bit + mask // bit, 2) * bit
        bit *= 2
    return found


def shifted(field, axis, step):
    size = field.shape[axis]
    index = lax.broadcasted_iota(jnp.int32, field.shape, axis)
    moved = pltpu.roll(field, 1 if step == 1 else size - 1, axis)
    return jnp.where(index == (0 if step == 1 else size - 1), 0.0, moved)


def coefficients(m):
    a0 = m[0] / m[1]
    rr1 = m[0] - 2.0 * a0 * m[1] + a0 * a0 * m[2]
    p10, p11 = 1.0 + rr1 / m[0], -a0
    a1 = rr1 / (p10 * p10 * m[1] + 2.0 * p10 * p11 * m[2] + p11 * p11 * m[3])
    r1, r2 = -a0 - a1 * p10, -a1 * p11
    rr2 = m[0] + r1 * r1 * m[2] + r2 * r2 * m[4] + 2.0 * (r1 * m[1] + r2 * m[2] + r1 * r2 * m[3])
    beta = rr2 / rr1
    p20, p21, p22 = 1.0 + beta * p10, r1 + beta * p11, r2
    bottom = (
        p20 * p20 * m[1]
        + p21 * p21 * m[3]
        + p22 * p22 * m[5]
        + 2.0 * (p20 * p21 * m[2] + p20 * p22 * m[3] + p21 * p22 * m[4])
    )
    a2 = rr2 / bottom
    return a0 + a1 * p10 + a2 * p20, a1 * p11 + a2 * p21, a2 * p22


def kernel(
    count,
    video_hbm, w_in_hbm, b_in_hbm, w_out_hbm, b_out_hbm, screen_hbm,
    recv2,
    video_ref, w_in_ref, b_in_ref, w_out_ref, b_out_ref, screen_ref, load_sem,
    wide, packed, send1, recv1, power0, power1, power2, power3, field1, field2, masks,
    mine, sums, send2,
    send1_sem, recv1_sem, sum_send_sem, sum_recv_sem, send2_sem, recv2_sem, local_sem,
):
    me = lax.axis_index("tm")
    chips = count // 2
    chip, core = lax.rem(me, chips), me // chips
    _, channels, rows, cols = video_ref.shape
    units = w_in_ref.shape[1]
    frames = count
    own = cols // chips
    half = rows // 2
    window = half + ITERS
    pitch = window + 2
    chunk = send1.shape[1]
    band = rows // count
    bands = count // 2

    barrier = pltpu.get_barrier_semaphore()

    def greet(step, carry):
        pl.semaphore_signal(barrier, inc=1, device_id={"tm": lax.rem(me + step, count)})
        return carry

    lax.fori_loop(1, count, greet, 0)

    loads = [
        pltpu.make_async_copy(source, dest, load_sem.at[i])
        for i, (source, dest) in enumerate(
            (
                (video_hbm, video_ref),
                (w_in_hbm, w_in_ref),
                (b_in_hbm, b_in_ref),
                (w_out_hbm, w_out_ref),
                (b_out_hbm, b_out_ref),
                (screen_hbm, screen_ref),
            )
        )
    ]
    for load in loads:
        load.start()
    for load in loads:
        load.wait()

    tiles = wide.shape[2] // LANES
    for c in range(channels):
        wide[c, :, :LANES] = jnp.zeros((rows, LANES), jnp.float32)
        for t in range(1 + cols // LANES, tiles):
            wide[c, :, t * LANES:(t + 1) * LANES] = jnp.zeros((rows, LANES), jnp.float32)
        wide[c, :, LANES:LANES + cols] = video_ref[0, c].astype(jnp.float32)
    lane2 = lax.broadcasted_iota(jnp.int32, (rows, LANES), 1)
    for k in range(chips):
        tile, offset = divmod(LANES + own * k - HALO, LANES)
        for c in range(channels):
            first = wide[c, :, tile * LANES:(tile + 1) * LANES]
            if offset:
                second = wide[c, :, (tile + 1) * LANES:(tile + 2) * LANES]
                first = pltpu.roll(first, LANES - offset, 1)
                second = pltpu.roll(second, LANES - offset, 1)
                first = jnp.where(lane2 < LANES - offset, first, second)
            field1[(k * channels + c) * rows:(k * channels + c + 1) * rows, :] = first
    packed[...] = jnp.zeros_like(packed)

    def grade(k):
        column = lane2 + (own * k - HALO)
        inside = jnp.logical_and(column >= 0, column < cols)
        parts = [[] for _ in range(channels)]
        for start, size in blocks_of(rows, 32):
            pixels = [
                field1[pl.ds(pl.multiple_of((k * channels + c) * rows + start, 8), size), :]
                for c in range(channels)
            ]
            total = [pixels[c] + b_out_ref[c] for c in range(channels)]
            for j in range(units):
                h = pixels[0] * (0.5 * w_in_ref[0, j]) + 0.5 * b_in_ref[j]
                for c in range(1, channels):
                    h = h + pixels[c] * (0.5 * w_in_ref[c, j])
                act = h * jnp.tanh(h) + h
                for c in range(channels):
                    total[c] = total[c] + act * w_out_ref[c, j]
            for c in range(channels):
                parts[c].append(total[c])
        for c in range(channels):
            graded = parts[c][0] if len(parts[c]) == 1 else jnp.concatenate(parts[c], 0)
            graded = jnp.where(inside, graded, 0.0)
            beside = shifted(graded, 0, 1) + shifted(graded, 0, -1)
            beside = beside + pltpu.roll(graded, 1, 1) + pltpu.roll(graded, LANES - 1, 1)
            target = jnp.where(inside, (screen_ref[c] + 4.0) * graded - beside, 0.0)
            first = c * pitch + 1
            packed[0, first:first + window, :] = target[:window]
            packed[1, first:first + window, :] = target[rows - window:]

    def copy1(dest):
        return pltpu.make_async_remote_copy(
            src_ref=send1.at[dest],
            dst_ref=recv1.at[me],
            send_sem=send1_sem.at[dest],
            recv_sem=recv1_sem.at[me],
            device_id={"tm": dest},
        )

    def arrival1(source):
        return pltpu.make_async_remote_copy(
            src_ref=send1.at[source],
            dst_ref=recv1.at[source],
            send_sem=send1_sem.at[source],
            recv_sem=recv1_sem.at[source],
            device_id={"tm": source},
        )

    held = min(HELD, chips - 1)

    def launch(k):
        for side in range(2):
            dest = side * chips + k

            @pl.when(dest != me)
            def _():
                copy1(dest).start()

    def make(step, carry):
        k = lax.rem(chip + chips // 2 + step, chips)
        grade(k)
        for side in range(2):
            send1[side * chips + k] = packed[side].astype(jnp.bfloat16)

        @pl.when(step == held)
        def _():
            pl.semaphore_wait(barrier, count - 1)
            for earlier in range(held):
                launch(lax.rem(chip + chips // 2 + earlier, chips))

        @pl.when(step >= held)
        def _():
            launch(k)

        return carry

    line = lax.broadcasted_iota(jnp.int32, (chunk, LANES), 0)
    lane = lax.broadcasted_iota(jnp.int32, (chunk, LANES), 1)
    column = lane + (own * chip - HALO)
    inside = jnp.logical_and(column >= 0, column < cols)
    owned = jnp.logical_and(lane >= HALO, lane < HALO + own)
    shift = core * ITERS
    weight = jnp.zeros((chunk, LANES), jnp.float32)
    kept = jnp.zeros((chunk, LANES), jnp.float32)
    for c in range(channels):
        rows_of = jnp.logical_and(line >= c * pitch + 1, line < c * pitch + 1 + window)
        kept = jnp.where(jnp.logical_and(rows_of, inside), 1.0, kept)
        weight = jnp.where(rows_of, 6.0 + screen_ref[c], weight)
        start = c * pitch + 1 + shift
        mine_of = jnp.logical_and(line >= start, line < start + half)
        masks[2 + c] = jnp.where(jnp.logical_and(mine_of, owned), 1.0, 0.0)
    masks[0] = weight
    masks[1] = kept

    lax.fori_loop(0, chips, make, 0)
    recv1[me] = send1[me]

    def within(field):
        total = pltpu.roll(field, 1, 0) + pltpu.roll(field, chunk - 1, 0)
        total = total + pltpu.roll(field, 1, 1) + pltpu.roll(field, LANES - 1, 1)
        return (masks[0] * field - total) * masks[1]

    def land(step, carry):
        k = lax.rem(chip + chips // 2 + chips - step, chips)
        near, far = core * chips + k, (1 - core) * chips + k

        @pl.when(near != me)
        def _():
            arrival1(near).wait_recv()

        arrival1(far).wait_recv()
        sources = (near, far)
        spots = [pl.ds(pl.multiple_of(source * chunk, chunk), chunk) for source in sources]
        fields = [recv1[source].astype(jnp.float32) for source in sources]
        for spot, field in zip(spots, fields):
            power0[spot, :] = field
        for power in (power1, power2, power3):
            fields = [within(field) for field in fields]
            for spot, field in zip(spots, fields):
                power[spot, :] = field
        return carry

    lax.fori_loop(0, chips, land, 0)

    def beside(terms, f):
        if f == 0:
            return terms[1]
        if f == frames - 1:
            return terms[f - 1]
        return terms[f - 1] + terms[f + 1]

    def moments(block, totals):
        def at(ref, f):
            return ref[pl.ds(pl.multiple_of(f * chunk + block * 8, 8), 8), :]

        p0, p1, p2, v1, g, e, v2, h = ({} for _ in range(8))
        acc = [jnp.zeros((8, LANES), jnp.float32) for _ in range(6)]
        p0[0], p1[0] = at(power0, 0), at(power1, 0)
        for t in range(frames + 2):
            if t < frames:
                if t + 1 < frames:
                    p0[t + 1], p1[t + 1] = at(power0, t + 1), at(power1, t + 1)
                p2[t] = at(power2, t)
                v1[t] = p1[t] - beside(p0, t)
                g[t] = p2[t] - beside(p1, t)
                e[t] = p2[t] + g[t]
                field1[pl.ds(pl.multiple_of(t * chunk + block * 8, 8), 8), :] = v1[t]
            u = t - 1
            if 0 <= u < frames:
                v2[u] = g[u] - beside(v1, u)
                h[u] = at(power3, u) - beside(e, u)
                field2[pl.ds(pl.multiple_of(u * chunk + block * 8, 8), 8), :] = v2[u]
            w = t - 2
            if 0 <= w < frames:
                v3 = h[w] - beside(v2, w)
                pairs = ((p0[w], p0[w]), (p0[w], v1[w]), (v1[w], v1[w]), (v1[w], v2[w]), (v2[w], v2[w]), (v2[w], v3))
                for i, (left, right) in enumerate(pairs):
                    acc[i] = acc[i] + left * right
        result = []
        for c in range(channels):
            mask = masks[2 + c, pl.ds(pl.multiple_of(block * 8, 8), 8), :]
            for i in range(6):
                result.append(totals[c * 6 + i] + mask * acc[i])
        return tuple(result)

    lane1 = lax.broadcasted_iota(jnp.int32, (1, LANES), 1)
    zero = jnp.zeros((8, LANES), jnp.float32)
    totals = lax.fori_loop(0, chunk // 8, moments, (zero,) * (6 * channels))
    row = jnp.zeros((1, LANES), jnp.float32)
    for c in range(channels):
        for i in range(6):
            value = jnp.sum(totals[c * 6 + i], axis=0, keepdims=True)
            value = jnp.sum(value, axis=1, keepdims=True)
            row = jnp.where(lane1 == c * 8 + i, value, row)
    mine[0] = row

    def sum_copy(other, slot):
        return pltpu.make_async_remote_copy(
            src_ref=mine.at[0],
            dst_ref=sums.at[slot],
            send_sem=sum_send_sem.at[other],
            recv_sem=sum_recv_sem.at[slot],
            device_id={"tm": other},
        )

    def tell(step, carry):
        other = partner(me, step, count)

        @pl.when(other != me)
        def _():
            sum_copy(other, me).start()

        return carry

    lax.fori_loop(0, count, tell, 0)
    sums[me] = mine[0]

    def turn(f, carry):
        here = pl.ds(pl.multiple_of(f * chunk, chunk), chunk)
        for field, turned in ((power0, power1), (field1, power2), (field2, power3)):
            turned[pl.ds(f, chunk, frames), :] = field[here, :]
        return carry

    lax.fori_loop(0, frames, turn, 0)

    def sent(step, carry):
        copy1(lax.rem(me + step, count)).wait_send()
        return carry

    lax.fori_loop(1, count, sent, 0)

    def hear(step, carry):
        other = lax.rem(me + step, count)
        sum_copy(other, other).wait_recv()
        return carry

    lax.fori_loop(1, count, hear, 0)
    total = sums[0]
    for other in range(1, count):
        total = total + sums[other]
    moment = [total if i == 0 else pltpu.roll(total, LANES - i, 1) for i in range(6)]
    weights = coefficients(moment)
    spread = [
        [jnp.sum(jnp.where(lane1 == c * 8, w, 0.0), axis=1, keepdims=True) for w in weights]
        for c in range(channels)
    ]

    def copy2(slot, dest, where):
        return pltpu.make_async_remote_copy(
            src_ref=send2.at[slot],
            dst_ref=recv2.at[where],
            send_sem=send2_sem.at[slot],
            recv_sem=recv2_sem.at[where],
            device_id={"tm": dest},
        )

    def give(step, carry):
        slot = step
        dest = core * bands + slot
        for c in range(channels):
            for r in range(band):
                first = (c * pitch + 1 + shift + slot * band + r) * frames
                here = pl.ds(pl.multiple_of(first, frames), frames)
                result = spread[c][0] * power1[here, :]
                result = result + spread[c][1] * power2[here, :]
                result = result + spread[c][2] * power3[here, :]
                send2[slot, c, r] = result.astype(jnp.bfloat16)

        @pl.when(dest != me)
        def _():
            copy2(slot, dest, chip).start()

        @pl.when(dest == me)
        def _():
            pltpu.make_async_copy(send2.at[slot], recv2.at[chip], local_sem.at[1]).start()

        return carry

    lax.fori_loop(0, bands, give, 0)

    def drain(step, carry):
        other = lax.rem(me + step, count)
        sum_copy(other, me).wait_send()
        return carry

    lax.fori_loop(1, count, drain, 0)

    def take(k, carry):
        giver = core * chips + k

        @pl.when(giver != me)
        def _():
            copy2(0, giver, k).wait_recv()

        @pl.when(giver == me)
        def _():
            pltpu.make_async_copy(send2.at[0], recv2.at[k], local_sem.at[1]).wait()

        return carry

    lax.fori_loop(0, chips, take, 0)
    def finish(slot, carry):
        dest = core * bands + slot

        @pl.when(dest != me)
        def _():
            copy2(slot, dest, chip).wait_send()

        return carry

    lax.fori_loop(0, bands, finish, 0)


def assemble(own, recv2, out_ref):
    frames, channels, band, cols = out_ref.shape
    for start, size in blocks_of(cols, LANES):
        column = start + lax.broadcasted_iota(jnp.int32, (frames, LANES), 1)
        for c in range(channels):
            for r in range(band):
                tile = jnp.zeros((frames, LANES), jnp.float32)
                for k in range(start // own, (start + size - 1) // own + 1):
                    piece = recv2[k, c, r].astype(jnp.float32)
                    turn = (own * k - HALO - start) % LANES
                    piece = pltpu.roll(piece, turn, 1) if turn else piece
                    tile = jnp.where(column >= own * k, piece, tile)
                out_ref[:, c, r, start:start + size] = tile[:, :size]


def shards(count, video, w_in, b_in, w_out, b_out, screen):
    _, channels, rows, cols = video.shape
    chips, band = count // 2, rows // count
    window = rows // 2 + ITERS
    chunk = -(-channels * (window + 2) // 16) * 16
    f32, bf16 = jnp.float32, jnp.bfloat16
    field = pltpu.VMEM((count * chunk, LANES), f32)
    dma = pltpu.SemaphoreType.DMA
    held = 4 * (6 * count * chunk + (2 + channels + count) * chunk)
    held = LANES * (held + 8 * channels * count * count)
    limit = min(60 << 20, max(24 << 20, held + (8 << 20)))
    out = pl.pallas_call(
        functools.partial(kernel, count),
        out_shape=jax.ShapeDtypeStruct((chips, channels, band, count, LANES), bf16),
        in_specs=[pl.BlockSpec(memory_space=pl.ANY)] * 6,
        out_specs=pl.BlockSpec(memory_space=pl.ANY),
        scratch_shapes=[
            pltpu.VMEM(video.shape, video.dtype),
            pltpu.SMEM(w_in.shape[::-1], f32),
            pltpu.SMEM(b_in.shape, f32),
            pltpu.SMEM(w_out.shape, f32),
            pltpu.SMEM(b_out.shape, f32),
            pltpu.SMEM(screen.shape, f32),
            dma((6,)),
            pltpu.VMEM((channels, rows, (-(-cols // LANES) + 2) * LANES), f32),
            pltpu.VMEM((2, chunk, LANES), f32),
            pltpu.VMEM((count, chunk, LANES), bf16),
            pltpu.VMEM((count, chunk, LANES), bf16),
            field, field, field, field, field, field,
            pltpu.VMEM((2 + channels, chunk, LANES), f32),
            pltpu.VMEM((1, 1, LANES), f32),
            pltpu.VMEM((count, 1, LANES), f32),
            pltpu.VMEM((count // 2, channels, band, count, LANES), bf16),
            dma((count,)), dma((count,)), dma((count,)), dma((count,)),
            dma((count // 2,)), dma((chips,)), dma((2,)),
        ],
        compiler_params=pltpu.CompilerParams(collective_id=0, has_side_effects=True, vmem_limit_bytes=limit),
    )(*[pltpu.with_memory_space_constraint(a, pltpu.HBM) for a in (video, w_in.T, b_in, w_out, b_out, screen)])
    return pl.pallas_call(
        functools.partial(assemble, cols // chips),
        out_shape=jax.ShapeDtypeStruct((count, channels, band, cols), f32),
        in_specs=[pl.BlockSpec(memory_space=pltpu.VMEM)],
        out_specs=pl.BlockSpec(memory_space=pltpu.VMEM),
        compiler_params=pltpu.CompilerParams(vmem_limit_bytes=8 << 20),
    )(out)


def solution(mesh):
    in_specs = (P(("video", "tm"), None, None, None), P(), P(), P(), P(), P())
    out_specs = P("video", None, "tm", None)
    body = functools.partial(shards, mesh.shape["tm"])
    return jax.shard_map(body, mesh=mesh, in_specs=in_specs, out_specs=out_specs, check_vma=False)
```
